32 devices in a mesh: req: 4 (over y, core), ad: 8 (over z, x).
Axes of the slice: x: 2, y: 2, z: 4, core: 2. Of those that a mesh axis runs over, the one named last changes fastest.
Arguments:
- residual: bfloat16 [256, 32, 1152], P(('req', 'ad')), may hold values from -16 to 16
- lengths: int32 [256], P(('req', 'ad')), may hold values from 1 to 32, 7168 in all
- adapter_ids: int32 [256], P(('req', 'ad')), may hold values from 0 to 31, as said below
- ffn_gain: float32 [1152], replicated, may hold values from 0.5 to 1.5
- w_gate_up: bfloat16 [2, 1152, 3072], replicated, may hold values from -0.1875 to 0.1875
- w_down: bfloat16 [3072, 1152], replicated, may hold values from -0.109375 to 0.109375
- adapter_input_first: bfloat16 [32, 32, 1152], P('ad'), may hold values from -0.1875 to 0.1875
- ad_out_b: bfloat16 [32, 2, 16, 3072], P('ad'), may hold values from -1.5 to 1.5
- ad_down_a: bfloat16 [32, 16, 3072], P('ad'), may hold values from -0.109375 to 0.109375
- adapter_down_second: bfloat16 [32, 16, 1152], P('ad'), may hold values from -1.5 to 1.5
- final_gain: float32 [1152], replicated, may hold values from 0.5 to 1.5
- head_weight: bfloat16 [1152, 32000], P(None, ('req', 'ad')), may hold values from -3 to 3
Outputs:
- layer_out: bfloat16 [256, 32, 1152], P(('req', 'ad'))
- log_probs: float32 [256, 32000], P(None, ('req', 'ad'))
The draws below stay inside these ranges and needn't reach their ends.
Inputs may be any that keep to these rules, and one draw needn't show every extreme that they name: `adapter_ids`: the 8 requests of one device (aligned blocks of 8 requests in order) use adapters whose indices divided by 4 are all different.
All inputs are finite; a program needn't handle non-finite values. No bound on the sum of `lengths` on one device may be relied on, other than what follows from the above.
Results may differ from the reference program's by a relative error of at most 0.0076.
Values may be sent and summed in bfloat16 or wider, within the bound.
A program may use at most 128 MiB of HBM per device.

```python
import math
import jax
import jax.numpy as jnp
import numpy as np
from jax import lax

D = 1152
FF = 3072
VOCAB = 32000
RANK = 16
AD_DEV = 4
REQ_DEV = 8
SEQ = 32
ADAPTERS = 32
REQS = 256


def draw_residual(key, part):
    rough_key = jax.random.fold_in(jax.random.fold_in(key, 3), 0)
    values = jnp.clip(jax.random.normal(rough_key, (REQS, SEQ, D), jnp.float32), -6.0, 6.0)
    return values.astype(jnp.bfloat16)


def draw_head_weight(key, part):
    entry_key = jax.random.fold_in(jax.random.fold_in(key, 5), 0)
    rising = 0.7 + 0.6 * jnp.arange(VOCAB, dtype=jnp.float32) / VOCAB
    base_scale = 3.0 / math.sqrt(D)
    values = jnp.clip(jax.random.normal(entry_key, (D, VOCAB), jnp.float32), -6.0, 6.0) * (base_scale * rising)[None, :]
    return values.astype(jnp.bfloat16)


def draw_adapter_ids(key, part):
    blocks = REQS // REQ_DEV
    holders = ADAPTERS // AD_DEV
    hot_key, score_key, order_key, used_key = jax.random.split(jax.random.fold_in(key, 9), 4)
    hot = (jax.random.permutation(hot_key, holders) < max(holders // 4, 1)).astype(jnp.int32)
    scores = jax.random.randint(score_key, (blocks, holders), 0, 1024) + 768 * hot[None, :]
    scores = scores * holders + jnp.arange(holders, dtype=jnp.int32)[None, :]
    unused_top, selected_factors = lax.top_k(scores, REQ_DEV)
    shuffle = jax.random.randint(order_key, (blocks, REQ_DEV), 0, 1 << 16) * REQ_DEV + jnp.arange(REQ_DEV, dtype=jnp.int32)[None, :]
    selected_factors = jnp.take_along_axis(selected_factors, jnp.argsort(shuffle, axis=1), axis=1)
    used_local = jax.random.randint(used_key, (blocks, REQ_DEV), 0, AD_DEV)
    named = selected_factors * AD_DEV + used_local
    return named.reshape(REQS).astype(jnp.int32)


def levels(rng, dims, pieces, least, top_value):
    level = 1.0
    for dim, shards_of in pieces:
        draws = jax.random.uniform(jax.random.fold_in(jax.random.fold_in(rng, 6), dim), (shards_of,), jnp.float32, least / len(pieces), top_value / len(pieces))
        level = level * jnp.repeat(jnp.exp(draws), dims[dim] // shards_of).reshape((-1,) + (1,) * (len(dims) - 1 - dim))
    return level


def split_up(number_of, total, bound, lean):
    portions = [(1 << 20) // math.isqrt(rank ** lean) + 1 for rank in range(2, number_of + 1)]
    rest, counts = total - bound - (number_of - 1), [1] * (number_of - 1)
    while rest > 0:
        free = [i for i in range(number_of - 1) if counts[i] < bound]
        whole, remaining = sum([portions[i] for i in free]), rest
        for i in free:
            more = min(bound - counts[i], max(1, remaining * portions[i] // whole), rest)
            counts[i] = counts[i] + more
            rest = rest - more
    return np.array([bound] + counts)


def uneven_parts(key, count, total, reach, skew):
    if count == 2:
        one = jax.random.randint(key, (), max(1, total - reach), min(reach, total - 1) + 1)
        return jnp.stack([one, total - one])
    sizes = jnp.asarray(split_up(count, total, reach, skew), jnp.int32)
    twos = (count - 1) // 2
    source_of, sink = sizes[1:1 + 2 * twos:2], sizes[2:2 + 2 * twos:2]
    margin = jnp.minimum(source_of - 1, reach - sink)
    passed = jax.random.randint(jax.random.fold_in(key, 1), (twos,), 0, 1 << 20) % (margin + 1)
    sizes = sizes.at[1:1 + 2 * twos:2].set(source_of - passed).at[2:2 + 2 * twos:2].set(sink + passed)
    return sizes[jax.random.permutation(jax.random.fold_in(key, 2), count)]


def scatter_about(key, extent, scale, most, cuts=(), kind=jnp.bfloat16):
    loudness = levels(key, extent, cuts, -0.22, 0.18) if cuts else 1.0
    drawn = jax.random.normal(key, extent, jnp.float32) * scale * loudness
    return jnp.minimum(jnp.maximum(drawn, -most), most).astype(kind)


def setup_inputs(seed: int = 0) -> dict:
    arg_keys = jax.random.split(jax.random.key(seed), 13)
    residual = draw_residual(jax.random.fold_in(arg_keys[12], 71), 0)
    lengths = uneven_parts(arg_keys[1], REQS, REQS * SEQ * 7 // 8, SEQ, 0).astype(jnp.int32)
    adapter_ids = draw_adapter_ids(jax.random.fold_in(arg_keys[12], 71), 0)
    ffn_gain = jnp.clip(1.0 + 0.1 * jax.random.normal(arg_keys[3], (D,), jnp.float32), 0.5, 1.5)
    w_gate_up = scatter_about(arg_keys[4], (2, D, FF), D ** -0.5, 0.1875)
    w_down = scatter_about(arg_keys[5], (FF, D), FF ** -0.5, 0.109375)
    adapter_input_first = scatter_about(arg_keys[6], (ADAPTERS, 2 * RANK, D), D ** -0.5, 0.1875, ((0, 8),))
    ad_out_b = scatter_about(arg_keys[7], (ADAPTERS, 2, RANK, FF), RANK ** -0.5, 1.5, ((0, 8),))
    ad_down_a = scatter_about(arg_keys[8], (ADAPTERS, RANK, FF), FF ** -0.5, 0.109375, ((0, 8),))
    adapter_down_second = scatter_about(arg_keys[9], (ADAPTERS, RANK, D), RANK ** -0.5, 1.5, ((0, 8),))
    final_gain = jnp.clip(1.0 + 0.1 * jax.random.normal(arg_keys[10], (D,), jnp.float32), 0.5, 1.5)
    head_weight = draw_head_weight(jax.random.fold_in(arg_keys[12], 71), 0)
    return {"residual": residual, "lengths": lengths, "adapter_ids": adapter_ids, "ffn_gain": ffn_gain, "w_gate_up": w_gate_up, "w_down": w_down, "adapter_input_first": adapter_input_first, "ad_out_b": ad_out_b, "ad_down_a": ad_down_a, "adapter_down_second": adapter_down_second, "final_gain": final_gain, "head_weight": head_weight}


epsilon = 1e-05

def reference(residual, lengths, adapter_ids, ffn_gain, w_gate_up, w_down, adapter_input_first, ad_out_b, ad_down_a, adapter_down_second, final_gain, head_weight):
    block = math.gcd(REQS, 64)
    blocks = REQS // block

    def layer_block(index):
        start = (index * block).astype(jnp.int32)
        stream = lax.dynamic_slice_in_dim(residual, start, block, 0).astype(jnp.float32)
        req_len = lax.dynamic_slice_in_dim(lengths, start, block, 0)
        selected_factors = lax.dynamic_slice_in_dim(adapter_ids, start, block, 0)
        normalized_rows = (stream * lax.rsqrt(lax.optimization_barrier(jnp.mean(stream * stream, axis=-1, keepdims=True)) + epsilon) * ffn_gain).astype(jnp.bfloat16)
        input_lowrank_state = jnp.einsum('foa,fxa->fox', normalized_rows.astype(jnp.float32), adapter_input_first[selected_factors].astype(jnp.float32)).astype(jnp.bfloat16)
        input_lowrank_state = input_lowrank_state.astype(jnp.float32).reshape(block, SEQ, 2, RANK)
        delta_gu = jnp.einsum('bsjk,bjkf->bsjf', input_lowrank_state, ad_out_b[selected_factors].astype(jnp.float32)).astype(jnp.bfloat16)
        delta_gu = lax.optimization_barrier(delta_gu).astype(jnp.float32)
        flat = normalized_rows.reshape(block * SEQ, D)
        gate = jnp.dot(flat, w_gate_up[0], preferred_element_type=jnp.float32).reshape(block, SEQ, FF) + delta_gu[:, :, 0]
        up_part = jnp.dot(flat, w_gate_up[1], preferred_element_type=jnp.float32).reshape(block, SEQ, FF) + delta_gu[:, :, 1]
        hidden = (jax.nn.silu(gate) * up_part).astype(jnp.bfloat16)
        down_lowrank_state = jnp.einsum('bsf,bkf->bsk', hidden.astype(jnp.float32), ad_down_a[selected_factors].astype(jnp.float32)).astype(jnp.bfloat16)
        down_correction = jnp.einsum('rtc,rca->rta', down_lowrank_state.astype(jnp.float32), adapter_down_second[selected_factors].astype(jnp.float32)).astype(jnp.bfloat16)
        down_correction = lax.optimization_barrier(down_correction).astype(jnp.float32)
        base_down = jnp.dot(hidden.reshape(block * SEQ, FF), w_down, preferred_element_type=jnp.float32).reshape(block, SEQ, D)
        mixed = stream + base_down + down_correction
        valid = jnp.arange(SEQ, dtype=jnp.int32)[None, :] < req_len[:, None]
        block_out = jnp.where(valid[:, :, None], mixed, jnp.zeros_like(mixed)).astype(jnp.bfloat16)
        last_index = (req_len - 1).astype(jnp.int32)[:, None, None]
        last_row = jnp.take_along_axis(block_out, last_index, axis=1)[:, 0, :].astype(jnp.float32)
        final = (last_row * lax.rsqrt(lax.optimization_barrier(jnp.mean(last_row * last_row, axis=-1, keepdims=True)) + epsilon) * final_gain).astype(jnp.bfloat16)
        return (block_out, final)
    outputs, finals = lax.map(layer_block, jnp.arange(blocks, dtype=jnp.int32))
    layer_out = outputs.reshape(REQS, SEQ, D)
    finals = finals.reshape(REQS, D)
    logits = jnp.dot(finals, head_weight, preferred_element_type=jnp.float32)
    highest = lax.optimization_barrier(jnp.max(logits, axis=1, keepdims=True))
    shifted = logits - highest
    log_probs = shifted - jnp.log(lax.optimization_barrier(jnp.sum(jnp.exp(shifted), axis=1, keepdims=True)))
    return (layer_out, log_probs)
```

```python
import functools

import jax
import jax.numpy as jnp
from jax import lax
from jax.experimental import pallas as pl
from jax.experimental.pallas import tpu as pltpu
from jax.sharding import PartitionSpec as P

epsilon = 1e-05
MESH = pl.DeviceIdType.MESH
VMEM_SPEC = pl.BlockSpec(memory_space=pltpu.VMEM)
SMEM_SPEC = pl.BlockSpec(memory_space=pltpu.SMEM)


def rms_scale(values, gain):
    mean_sq = jnp.mean(values * values, axis=-1, keepdims=True)
    return values * lax.rsqrt(mean_sq + epsilon) * gain


def dispatch_kernel(
    groups, per_dev, ids_ref, len_ref, x_ref, rows_ref, meta_ref,
    stage, mstage, local_sem, send_sem, recv_sem, msend_sem, mrecv_sem,
):
    q = lax.axis_index("req")
    me = lax.axis_index("ad")
    n_req = x_ref.shape[0]
    barrier = pltpu.get_barrier_semaphore()

    def greet(k, carry):
        pl.semaphore_signal(
            barrier, inc=1, device_id=(q, lax.rem(me + k, groups)), device_id_type=MESH
        )
        return carry

    lax.fori_loop(1, groups, greet, 0)
    lane = lax.broadcasted_iota(jnp.int32, (8, 128), 1)

    def fill(h, carry):
        pick = jnp.int32(-1)
        code = jnp.int32(0)
        size = jnp.int32(0)
        for r in range(n_req):
            a = ids_ref[r]
            hit = lax.div(a, per_dev) == h
            pick = jnp.where(hit, r, pick)
            code = jnp.where(hit, lax.rem(a, per_dev), code)
            size = jnp.where(hit, len_ref[r], size)
        stage[h] = x_ref[jnp.maximum(pick, 0)]
        mstage[h] = jnp.where(lane == 0, code, jnp.where(lane == 1, size, pick))
        return carry

    lax.fori_loop(0, groups, fill, 0)
    own = pltpu.make_async_copy(stage.at[me], rows_ref.at[me], local_sem.at[0])
    own_meta = pltpu.make_async_copy(mstage.at[me], meta_ref.at[me], local_sem.at[1])
    own.start()
    own_meta.start()
    pl.semaphore_wait(barrier, groups - 1)

    def pair(k):
        h = lax.rem(me + k, groups)
        rows = pltpu.make_async_remote_copy(
            src_ref=stage.at[h], dst_ref=rows_ref.at[me],
            send_sem=send_sem.at[k], recv_sem=recv_sem.at[k],
            device_id=(q, h), device_id_type=MESH,
        )
        meta = pltpu.make_async_remote_copy(
            src_ref=mstage.at[h], dst_ref=meta_ref.at[me],
            send_sem=msend_sem.at[k], recv_sem=mrecv_sem.at[k],
            device_id=(q, h), device_id_type=MESH,
        )
        return rows, meta

    def start(k, carry):
        rows, meta = pair(k)
        meta.start()
        rows.start()
        return carry

    def finish(k, carry):
        rows, meta = pair(k)
        meta.wait()
        rows.wait()
        return carry

    lax.fori_loop(1, groups, start, 0)
    lax.fori_loop(1, groups, finish, 0)
    own.wait()
    own_meta.wait()


def dispatch(residual, lengths, adapter_ids, groups, per_dev):
    n_req, seq, width = residual.shape
    dma = pltpu.SemaphoreType.DMA
    return pl.pallas_call(
        functools.partial(dispatch_kernel, groups, per_dev),
        out_shape=(
            jax.ShapeDtypeStruct((groups, seq, width), residual.dtype),
            jax.ShapeDtypeStruct((groups, 8, 128), jnp.int32),
        ),
        in_specs=[SMEM_SPEC, SMEM_SPEC, VMEM_SPEC],
        out_specs=(VMEM_SPEC, VMEM_SPEC),
        scratch_shapes=[
            pltpu.VMEM((groups, seq, width), residual.dtype),
            pltpu.VMEM((groups, 8, 128), jnp.int32),
            dma((2,)), dma((groups,)), dma((groups,)), dma((groups,)), dma((groups,)),
        ],
        compiler_params=pltpu.CompilerParams(
            collective_id=0, has_side_effects=True, vmem_limit_bytes=16 << 20
        ),
    )(adapter_ids, lengths, residual)


def head_kernel(
    n_req_axis, groups, per_dev, ids_ref, fin_ref, y_ref, w_ref, out_ref, lp_ref,
    gathered, wide, back, stats, own_stats, local_sem,
    fsend, frecv, ysend, yrecv, ssend, srecv,
):
    q = lax.axis_index("req")
    a = lax.axis_index("ad")
    n = n_req_axis * groups
    me = q * groups + a
    n_req = out_ref.shape[0]
    width = out_ref.shape[2]
    total_req = lp_ref.shape[0]
    slots = n * groups
    barrier = pltpu.get_barrier_semaphore()

    def target(k):
        t = lax.rem(me + k, n)
        return (lax.div(t, groups), lax.rem(t, groups))

    def greet(k, carry):
        pl.semaphore_signal(barrier, inc=1, device_id=target(k), device_id_type=MESH)
        return carry

    lax.fori_loop(1, n, greet, 0)
    gathered[me] = fin_ref[...]
    own = pltpu.make_async_copy(y_ref.at[a], back.at[a], local_sem)
    own.start()
    pl.semaphore_wait(barrier, n - 1)

    def fin_copy(k):
        return pltpu.make_async_remote_copy(
            src_ref=fin_ref, dst_ref=gathered.at[me],
            send_sem=fsend.at[k], recv_sem=frecv.at[k],
            device_id=target(k), device_id_type=MESH,
        )

    def row_copy(k):
        h = lax.rem(a + k, groups)
        return pltpu.make_async_remote_copy(
            src_ref=y_ref.at[h], dst_ref=back.at[a],
            send_sem=ysend.at[k], recv_sem=yrecv.at[k],
            device_id=(q, h), device_id_type=MESH,
        )

    def stat_copy(k):
        return pltpu.make_async_remote_copy(
            src_ref=own_stats, dst_ref=stats.at[me],
            send_sem=ssend.at[k], recv_sem=srecv.at[k],
            device_id=target(k), device_id_type=MESH,
        )

    def start_all(copy, count):
        def body(k, carry):
            copy(k).start()
            return carry
        lax.fori_loop(1, count, body, 0)

    def wait_all(copy, count):
        def body(k, carry):
            copy(k).wait()
            return carry
        lax.fori_loop(1, count, body, 0)

    start_all(fin_copy, n)
    start_all(row_copy, groups)
    wait_all(fin_copy, n)

    def widen(d, carry):
        at = pl.multiple_of(d * groups, 8)
        wide[pl.ds(at, groups), :] = gathered[d].astype(jnp.float32)
        return carry

    lax.fori_loop(0, n, widen, 0)
    picked = jnp.transpose(wide[:, width:])[0:1, :].astype(jnp.int32)
    slot = lax.broadcasted_iota(jnp.int32, (1, slots), 1)
    req_of = lax.div(slot, groups * groups)
    source = lax.rem(slot, groups)
    row_id = (req_of * groups + source) * n_req + picked
    row_id = jnp.where(picked >= 0, row_id, -1)
    want = lax.broadcasted_iota(jnp.int32, (total_req, slots), 0)
    place = jnp.where(want == row_id, 1.0, 0.0).astype(jnp.bfloat16)
    ordered = jnp.dot(
        place, wide[:, :width].astype(jnp.bfloat16), preferred_element_type=jnp.float32
    ).astype(jnp.bfloat16)
    logits = jnp.dot(ordered, w_ref[...], preferred_element_type=jnp.float32)
    lp_ref[...] = logits
    top = jnp.max(logits, axis=1, keepdims=True)
    part = jnp.sum(jnp.exp(logits - top), axis=1, keepdims=True)
    own_stats[0:1, :] = jnp.transpose(jnp.broadcast_to(top, (total_req, 128)))[0:1, :]
    own_stats[1:2, :] = jnp.transpose(jnp.broadcast_to(part, (total_req, 128)))[0:1, :]
    start_all(stat_copy, n)
    stats[me] = own_stats[...]

    wait_all(row_copy, groups)
    own.wait()
    for r in range(n_req):
        out_ref[r] = back[lax.div(ids_ref[r], per_dev)]

    wait_all(stat_copy, n)
    tops = stats[:, 0, :]
    best = jnp.max(tops, axis=0, keepdims=True)
    total = jnp.sum(stats[:, 1, :] * jnp.exp(tops - best), axis=0, keepdims=True)
    best_col = jnp.transpose(jnp.broadcast_to(best, (128, total_req)))[:, 0:1]
    log_col = jnp.transpose(jnp.broadcast_to(jnp.log(total), (128, total_req)))[:, 0:1]
    lp_ref[...] = lp_ref[...] - best_col - log_col


def head(adapter_ids, final, y, head_weight, n_req, total_req, n_req_axis, groups, per_dev):
    n = n_req_axis * groups
    seq, width = y.shape[1:]
    dma = pltpu.SemaphoreType.DMA
    return pl.pallas_call(
        functools.partial(head_kernel, n_req_axis, groups, per_dev),
        out_shape=(
            jax.ShapeDtypeStruct((n_req, seq, width), y.dtype),
            jax.ShapeDtypeStruct((total_req, head_weight.shape[1]), jnp.float32),
        ),
        in_specs=[SMEM_SPEC, VMEM_SPEC, VMEM_SPEC, VMEM_SPEC],
        out_specs=(VMEM_SPEC, VMEM_SPEC),
        scratch_shapes=[
            pltpu.VMEM((n, groups, width + 128), jnp.bfloat16),
            pltpu.VMEM((n * groups, width + 128), jnp.float32),
            pltpu.VMEM((groups, seq, width), y.dtype),
            pltpu.VMEM((n, 2, total_req), jnp.float32),
            pltpu.VMEM((2, total_req), jnp.float32),
            dma(()), dma((n,)), dma((n,)), dma((groups,)), dma((groups,)), dma((n,)), dma((n,)),
        ],
        compiler_params=pltpu.CompilerParams(
            collective_id=1, has_side_effects=True, vmem_limit_bytes=56 << 20
        ),
    )(adapter_ids, final, y, head_weight)


def local(
    residual,
    lengths,
    adapter_ids,
    ffn_gain,
    w_gate_up,
    w_down,
    adapter_input_first,
    ad_out_b,
    ad_down_a,
    adapter_down_second,
    final_gain,
    head_weight,
):
    n_req, seq, width = residual.shape
    groups = lax.axis_size("ad")
    n_req_axis = lax.axis_size("req")
    per_dev = adapter_input_first.shape[0]
    rank = ad_down_a.shape[1]
    units = w_down.shape[0]
    f32 = jnp.float32
    rows, meta = dispatch(residual, lengths, adapter_ids, groups, per_dev)
    slot_id = meta[:, 0, 0]
    slot_len = meta[:, 0, 1]
    slot_req = meta[:, 0, 2]
    positions = jnp.arange(seq, dtype=jnp.int32)
    flat = rows.reshape(groups * seq, width)
    row_id = jnp.repeat(slot_id, seq)[:, None]
    valid = (positions[None, :] < slot_len[:, None]).reshape(groups * seq, 1)
    stream = flat.astype(f32)
    normed = rms_scale(stream, ffn_gain).astype(jnp.bfloat16)
    in_a = adapter_input_first.reshape(per_dev * 2 * rank, width)
    low = lax.dot_general(normed, in_a, (((1,), (1,)), ((), ())), preferred_element_type=f32)
    lane = jnp.arange(per_dev * 2 * rank, dtype=jnp.int32)[None, :]
    mine = lane // (2 * rank) == row_id
    half = lane % (2 * rank) < rank
    low_gate = jnp.where(mine & half, low, 0.0).astype(jnp.bfloat16)
    low_up = jnp.where(mine & ~half, low, 0.0).astype(jnp.bfloat16)
    out_b = ad_out_b.reshape(per_dev * 2 * rank, units)

    def widened(base, lowered):
        return jnp.dot(normed, base, preferred_element_type=f32) + jnp.dot(
            lowered, out_b, preferred_element_type=f32
        )

    gate = widened(w_gate_up[0], low_gate)
    up_part = widened(w_gate_up[1], low_up)
    hidden = (jax.nn.silu(gate) * up_part).astype(jnp.bfloat16)
    down_a = ad_down_a.reshape(per_dev * rank, units)
    low_d = lax.dot_general(hidden, down_a, (((1,), (1,)), ((), ())), preferred_element_type=f32)
    lane_d = jnp.arange(per_dev * rank, dtype=jnp.int32)[None, :]
    low_d = jnp.where(lane_d // rank == row_id, low_d, 0.0).astype(jnp.bfloat16)
    mixed = (
        stream
        + jnp.dot(hidden, w_down, preferred_element_type=f32)
        + jnp.dot(low_d, adapter_down_second.reshape(per_dev * rank, width), preferred_element_type=f32)
    )
    y = jnp.where(valid, mixed, 0.0).astype(jnp.bfloat16).reshape(groups, seq, width)
    is_last = (positions[None, :] == slot_len[:, None] - 1)[..., None]
    last = jnp.sum(jnp.where(is_last, y.astype(f32), 0.0), axis=1)
    final = rms_scale(last, final_gain).astype(jnp.bfloat16)
    tag = jnp.broadcast_to(slot_req[:, None], (groups, 128)).astype(jnp.bfloat16)
    final = jnp.concatenate([final, tag], axis=1)
    return head(
        adapter_ids, final, y, head_weight, n_req, n_req * n_req_axis * groups,
        n_req_axis, groups, per_dev,
    )


def solution(mesh):
    in_specs = (
        P(("req", "ad"), None, None),
        P(("req", "ad")),
        P(("req", "ad")),
        P(),
        P(),
        P(),
        P("ad", None, None),
        P("ad", None, None, None),
        P("ad", None, None),
        P("ad", None, None),
        P(),
        P(None, ("req", "ad")),
    )
    out_specs = (P(("req", "ad"), None, None), P(None, ("req", "ad")))
    return jax.shard_map(local, mesh=mesh, in_specs=in_specs, out_specs=out_specs, check_vma=False)
```

```python
import functools

import jax
import jax.numpy as jnp
from jax import lax
from jax.experimental import pallas as pl
from jax.experimental.pallas import tpu as pltpu
from jax.sharding import PartitionSpec as P

epsilon = 1e-05
CHUNKS = 1
MESH = pl.DeviceIdType.MESH
VMEM_SPEC = pl.BlockSpec(memory_space=pltpu.VMEM)
ANY_SPEC = pl.BlockSpec(memory_space=pl.ANY)
NT = (((1,), (1,)), ((), ()))


def layer_kernel(
    n_q, groups, per_dev, n_req,
    ids_hbm, len_hbm, x_hbm, gain_ref, fgain_ref, wgu_hbm, wd_hbm, ina_hbm, outb_hbm,
    downa_hbm, downb_hbm, wh_hbm,
    back, lt_ref, lse_ref,
    ids, lens, xs, stage, mstage, recv, mrecv, normed, low_g, low_u, hidden, mixed, y, last,
    wgu, wd, ina, outb, downa, downb, wh,
    fin, gathered, wide, stats, own_stats,
    isem, wsem, lsem, rsend, rrecv, msend, mrec, ysend, yrecv,
    fsend, frecv, gsend, grecv, ssend, srecv,
):
    f32 = jnp.float32
    bf16 = jnp.bfloat16
    q = lax.axis_index("req")
    a = lax.axis_index("ad")
    n = n_q * groups
    me = q * groups + a
    seq, width = xs.shape[1:]
    rank = downa.shape[0] // per_dev
    units = wd.shape[0]
    slots = n * groups
    total_req = n * n_req
    barrier = pltpu.get_barrier_semaphore()

    def target(k):
        t = lax.rem(me + k, n)
        return (lax.div(t, groups), lax.rem(t, groups))

    firsts = [
        pltpu.make_async_copy(ids_hbm, ids, isem.at[0]),
        pltpu.make_async_copy(len_hbm, lens, isem.at[1]),
        pltpu.make_async_copy(x_hbm, xs, isem.at[2]),
    ]
    for copy in firsts:
        copy.start()

    def greet(k, carry):
        pl.semaphore_signal(barrier, inc=1, device_id=target(k), device_id_type=MESH)
        return carry

    lax.fori_loop(1, n, greet, 0)
    part = width // 4
    loads = [pltpu.make_async_copy(ina_hbm, ina, wsem.at[0])]
    for j in range(2):
        for c in range(4):
            rows = pl.ds(c * part, part)
            loads.append(
                pltpu.make_async_copy(
                    wgu_hbm.at[j, rows], wgu.at[j, rows], wsem.at[1 + 4 * j + c]
                )
            )
    loads.append(pltpu.make_async_copy(outb_hbm, outb, wsem.at[9]))
    early = len(loads)
    loads.append(pltpu.make_async_copy(downa_hbm, downa, wsem.at[10]))
    loads.append(pltpu.make_async_copy(downb_hbm, downb, wsem.at[11]))
    for c in range(2):
        rows = pl.ds(c * (units // 2), units // 2)
        loads.append(pltpu.make_async_copy(wd_hbm.at[rows], wd.at[rows], wsem.at[12 + c]))
    later = len(loads)
    loads.append(pltpu.make_async_copy(wh_hbm, wh, wsem.at[14]))
    for copy in firsts:
        copy.wait()
    for copy in loads:
        copy.start()

    line = lax.broadcasted_iota(jnp.int32, (8, 128), 0)

    def fill(k, carry):
        h = lax.rem(a + k, groups)
        pick = jnp.int32(-1)
        code = jnp.int32(0)
        size = jnp.int32(0)
        for r in range(n_req):
            i = ids[r]
            hit = lax.div(i, per_dev) == h
            pick = jnp.where(hit, r, pick)
            code = jnp.where(hit, lax.rem(i, per_dev), code)
            size = jnp.where(hit, lens[r], size)
        stage[k] = xs[jnp.maximum(pick, 0)]
        mstage[k] = jnp.where(line == 0, code, jnp.where(line == 1, size, pick))
        return carry

    lax.fori_loop(0, groups, fill, 0)
    pl.semaphore_wait(barrier, n - 1)

    def row_copy(k):
        return pltpu.make_async_remote_copy(
            src_ref=stage.at[k], dst_ref=recv.at[k],
            send_sem=rsend.at[k], recv_sem=rrecv.at[k],
            device_id=(q, lax.rem(a + k, groups)), device_id_type=MESH,
        )

    def meta_copy(k):
        return pltpu.make_async_remote_copy(
            src_ref=mstage.at[k], dst_ref=mrecv.at[k],
            send_sem=msend.at[k], recv_sem=mrec.at[k],
            device_id=(q, lax.rem(a + k, groups)), device_id_type=MESH,
        )

    def back_copy(k):
        return pltpu.make_async_remote_copy(
            src_ref=y.at[k], dst_ref=back.at[a],
            send_sem=ysend.at[k], recv_sem=yrecv.at[k],
            device_id=(q, lax.rem(a + groups - k, groups)), device_id_type=MESH,
        )

    def start_rows(k, carry):
        meta_copy(k).start()
        row_copy(k).start()
        return carry

    lax.fori_loop(1, groups, start_rows, 0)
    recv[0] = stage[0]
    mrecv[0] = mstage[0]
    gain = gain_ref[...].reshape(1, width)
    lane = lax.broadcasted_iota(jnp.int32, (seq, per_dev * 2 * rank), 1)
    lane_d = lax.broadcasted_iota(jnp.int32, (seq, per_dev * rank), 1)
    group_of = lax.div(lane, 2 * rank)
    is_gate = lax.rem(lane, 2 * rank) < rank
    row_at = lax.broadcasted_iota(jnp.int32, (seq, width), 0)
    per = groups // CHUNKS
    size = per * seq
    tile_f = 512
    tile_d = width // 3
    own_back = pltpu.make_async_copy(y.at[0], back.at[a], lsem)

    for chunk in range(CHUNKS):
        mine = range(chunk * per, (chunk + 1) * per)
        for s in mine:
            if s > 0:
                meta_copy(s).wait_recv()
                row_copy(s).wait_recv()
            v = recv[s].astype(f32)
            mean_sq = jnp.mean(v * v, axis=-1, keepdims=True)
            at = (s - chunk * per) * seq
            normed[at : at + seq, :] = (v * lax.rsqrt(mean_sq + epsilon) * gain).astype(bf16)
        if chunk == 0:
            for copy in loads[:early]:
                copy.wait()
        low = lax.dot_general(normed[...], ina[...], NT, preferred_element_type=f32)
        for s in mine:
            at = (s - chunk * per) * seq
            here = group_of == mrecv[s, 0:1, : lane.shape[1]]
            piece = low[at : at + seq]
            low_g[at : at + seq, :] = jnp.where(here & is_gate, piece, 0.0).astype(bf16)
            low_u[at : at + seq, :] = jnp.where(
                here & jnp.logical_not(is_gate), piece, 0.0
            ).astype(bf16)

        def units_step(j, carry):
            cols = pl.ds(pl.multiple_of(j * tile_f, tile_f), tile_f)
            gate = jnp.dot(normed[...], wgu[0, :, cols], preferred_element_type=f32)
            gate = gate + jnp.dot(low_g[...], outb[:, cols], preferred_element_type=f32)
            up = jnp.dot(normed[...], wgu[1, :, cols], preferred_element_type=f32)
            up = up + jnp.dot(low_u[...], outb[:, cols], preferred_element_type=f32)
            hidden[:, cols] = (gate / (1.0 + jnp.exp(-gate)) * up).astype(bf16)
            return carry

        lax.fori_loop(0, units // tile_f, units_step, 0)
        if chunk == 0:
            for copy in loads[early:later]:
                copy.wait()
        low_d = lax.dot_general(hidden[...], downa[...], NT, preferred_element_type=f32)
        pieces = []
        for s in mine:
            at = (s - chunk * per) * seq
            here = lax.div(lane_d, rank) == mrecv[s, 0:1, : lane_d.shape[1]]
            pieces.append(jnp.where(here, low_d[at : at + seq], 0.0))
        low_d = jnp.concatenate(pieces, axis=0).astype(bf16)
        low_g[:, : lane_d.shape[1]] = low_d

        def width_step(j, carry):
            cols = pl.ds(pl.multiple_of(j * tile_d, tile_d), tile_d)
            mixed[:, cols] = jnp.dot(
                hidden[...], wd[:, cols], preferred_element_type=f32
            ) + jnp.dot(
                low_g[:, : lane_d.shape[1]], downb[:, cols], preferred_element_type=f32
            )
            return carry

        lax.fori_loop(0, width // tile_d, width_step, 0)
        for s in mine:
            at = (s - chunk * per) * seq
            length = mrecv[s, 1:2, 0:1]
            total = recv[s].astype(f32) + mixed[at : at + seq, :]
            out = jnp.where(row_at < length, total, 0.0).astype(bf16)
            y[s] = out
            last[s : s + 1, :width] = jnp.sum(
                jnp.where(row_at == length - 1, out.astype(f32), 0.0), axis=0, keepdims=True
            )
            last[s : s + 1, width:] = mrecv[s, 2:3, :].astype(f32)
        if chunk < CHUNKS - 1:
            for s in mine:
                if s > 0:
                    back_copy(s).start()
                else:
                    own_back.start()

    rows = last[:, :width]
    mean_sq = jnp.mean(rows * rows, axis=-1, keepdims=True)
    fin[:, :width] = (rows * lax.rsqrt(mean_sq + epsilon) * fgain_ref[...].reshape(1, width)).astype(bf16)
    fin[:, width:] = last[:, width:].astype(bf16)
    gathered[me] = fin[...]

    half = n // 2
    pairs = n_q // 2
    core = lax.rem(q, 2)
    sibling = (q + 1 - 2 * core, a)
    place_me = lax.div(q, 2) * groups + a

    def far(k):
        t = lax.rem(place_me + k, half)
        return (2 * lax.div(t, groups) + core, lax.rem(t, groups))

    def fin_copy(k):
        return pltpu.make_async_remote_copy(
            src_ref=fin, dst_ref=gathered.at[me],
            send_sem=fsend.at[k], recv_sem=frecv.at[k],
            device_id=far(k), device_id_type=MESH,
        )

    def pass_on(k):
        t = lax.rem(place_me + half - k, half)
        origin = (2 * lax.div(t, groups) + core) * groups + lax.rem(t, groups)
        return pltpu.make_async_remote_copy(
            src_ref=gathered.at[origin], dst_ref=gathered.at[origin],
            send_sem=gsend.at[k], recv_sem=grecv.at[k],
            device_id=sibling, device_id_type=MESH,
        )

    def stat_copy(k):
        return pltpu.make_async_remote_copy(
            src_ref=own_stats, dst_ref=stats.at[me],
            send_sem=ssend.at[k], recv_sem=srecv.at[k],
            device_id=target(k), device_id_type=MESH,
        )

    def each(low_k, high_k, action):
        def body(k, carry):
            action(k)
            return carry
        lax.fori_loop(low_k, high_k, body, 0)

    each(1, half, lambda k: fin_copy(k).start())
    pass_on(0).start()
    for s in range((CHUNKS - 1) * per, groups):
        if s > 0:
            back_copy(s).start()
        else:
            own_back.start()

    def relay(k):
        fin_copy(k).wait_recv()
        pass_on(k).start()

    each(1, half, relay)
    each(0, half, lambda k: pass_on(k).wait_recv())

    def widen(d):
        at = pl.multiple_of(d * groups, 8)
        wide[pl.ds(at, groups), :] = gathered[d].astype(f32)

    each(0, n, widen)
    picked = jnp.transpose(wide[:, width:])[0:1, :].astype(jnp.int32)
    slot = lax.broadcasted_iota(jnp.int32, (1, slots), 1)
    device = lax.div(slot, groups)
    holder = lax.rem(device, groups)
    source = lax.rem(holder + groups - lax.rem(slot, groups), groups)
    row_id = (lax.div(device, groups) * groups + source) * n_req + picked
    row_id = jnp.where(picked >= 0, row_id, -1)
    want = lax.broadcasted_iota(jnp.int32, (total_req, slots), 0)
    place = jnp.where(want == row_id, 1.0, 0.0).astype(bf16)
    ordered = jnp.dot(
        place, wide[:, :width].astype(bf16), preferred_element_type=f32
    ).astype(bf16)
    loads[later].wait()
    logits = lax.dot_general(wh[...], ordered, NT, preferred_element_type=f32)
    lt_ref[...] = logits
    top = jnp.max(logits, axis=0, keepdims=True)
    own_stats[0:1, :] = top
    own_stats[1:2, :] = jnp.sum(jnp.exp(logits - top), axis=0, keepdims=True)
    each(1, n, lambda k: stat_copy(k).start())
    stats[me] = own_stats[...]

    def settle(k):
        row_copy(k).wait_send()
        meta_copy(k).wait_send()
        back_copy(k).wait()

    each(1, groups, settle)
    own_back.wait()
    each(1, half, lambda k: fin_copy(k).wait_send())
    each(0, half, lambda k: pass_on(k).wait_send())
    each(1, n, lambda k: stat_copy(k).wait())
    tops = stats[:, 0, :]
    best = jnp.max(tops, axis=0, keepdims=True)
    total = jnp.sum(stats[:, 1, :] * jnp.exp(tops - best), axis=0, keepdims=True)
    lse_ref[...] = best + jnp.log(total)


def local(
    residual,
    lengths,
    adapter_ids,
    ffn_gain,
    w_gate_up,
    w_down,
    adapter_input_first,
    ad_out_b,
    ad_down_a,
    adapter_down_second,
    final_gain,
    head_weight,
):
    n_req, seq, width = residual.shape
    groups = lax.axis_size("ad")
    n_q = lax.axis_size("req")
    n = n_q * groups
    per_dev = adapter_input_first.shape[0]
    rank = ad_down_a.shape[1]
    units = w_down.shape[0]
    shard = head_weight.shape[1]
    total_req = n * n_req
    rows = groups // CHUNKS * seq
    f32 = jnp.float32
    bf16 = jnp.bfloat16
    ina = adapter_input_first.reshape(per_dev * 2 * rank, width)
    outb = ad_out_b.reshape(per_dev * 2 * rank, units)
    downa = ad_down_a.reshape(per_dev * rank, units)
    downb = adapter_down_second.reshape(per_dev * rank, width)
    head_t = head_weight.T
    dma = pltpu.SemaphoreType.DMA
    vm = pltpu.VMEM
    back, logits_t, lse = pl.pallas_call(
        functools.partial(layer_kernel, n_q, groups, per_dev, n_req),
        out_shape=(
            jax.ShapeDtypeStruct((groups, seq, width), bf16),
            jax.ShapeDtypeStruct((shard, total_req), f32),
            jax.ShapeDtypeStruct((1, total_req), f32),
        ),
        in_specs=[ANY_SPEC] * 3 + [VMEM_SPEC] * 2 + [ANY_SPEC] * 7,
        out_specs=(VMEM_SPEC,) * 3,
        scratch_shapes=[
            pltpu.SMEM((n_req,), jnp.int32),
            pltpu.SMEM((n_req,), jnp.int32),
            vm((n_req, seq, width), bf16),
            vm((groups, seq, width), bf16),
            vm((groups, 8, 128), jnp.int32),
            vm((groups, seq, width), bf16),
            vm((groups, 8, 128), jnp.int32),
            vm((rows, width), bf16),
            vm((rows, per_dev * 2 * rank), bf16),
            vm((rows, per_dev * 2 * rank), bf16),
            vm((rows, units), bf16),
            vm((rows, width), f32),
            vm((groups, seq, width), bf16),
            vm((groups, width + 128), f32),
            vm(w_gate_up.shape, bf16),
            vm(w_down.shape, bf16),
            vm(ina.shape, bf16),
            vm(outb.shape, bf16),
            vm(downa.shape, bf16),
            vm(downb.shape, bf16),
            vm(head_t.shape, bf16),
            vm((groups, width + 128), bf16),
            vm((n, groups, width + 128), bf16),
            vm((n * groups, width + 128), f32),
            vm((n, 2, total_req), f32),
            vm((2, total_req), f32),
            dma((3,)), dma((15,)), dma(()),
            dma((groups,)), dma((groups,)), dma((groups,)), dma((groups,)),
            dma((groups,)), dma((groups,)),
            dma((n // 2,)), dma((n // 2,)), dma((n // 2,)), dma((n // 2,)),
            dma((n,)), dma((n,)),
        ],
        compiler_params=pltpu.CompilerParams(
            collective_id=0, has_side_effects=True, vmem_limit_bytes=60 << 20
        ),
    )(
        adapter_ids, lengths, residual, ffn_gain, final_gain, w_gate_up, w_down,
        ina, outb, downa, downb, head_t,
    )
    holder = adapter_ids // per_dev
    place = (holder[:, None] == jnp.arange(groups, dtype=jnp.int32)[None, :]).astype(bf16)
    layer_out = jnp.einsum("rh,hsf->rsf", place, back, preferred_element_type=f32).astype(bf16)
    return layer_out, (logits_t - lse).T


def solution(mesh):
    in_specs = (
        P(("req", "ad"), None, None),
        P(("req", "ad")),
        P(("req", "ad")),
        P(),
        P(),
        P(),
        P("ad", None, None),
        P("ad", None, None, None),
        P("ad", None, None),
        P("ad", None, None),
        P(),
        P(None, ("req", "ad")),
    )
    out_specs = (P(("req", "ad"), None, None), P(None, ("req", "ad")))
    return jax.shard_map(local, mesh=mesh, in_specs=in_specs, out_specs=out_specs, check_vma=False)
```

```python
import functools

import jax
import jax.numpy as jnp
from jax import lax
from jax.experimental import pallas as pl
from jax.experimental.pallas import tpu as pltpu
from jax.sharding import PartitionSpec as P

epsilon = 1e-05
CHUNKS = 2
MESH = pl.DeviceIdType.MESH
VMEM_SPEC = pl.BlockSpec(memory_space=pltpu.VMEM)
ANY_SPEC = pl.BlockSpec(memory_space=pl.ANY)
NT = (((1,), (1,)), ((), ()))


def layer_kernel(
    n_q, groups, per_dev, n_req,
    ids_hbm, len_hbm, x_hbm, gain_ref, fgain_ref, wgu_hbm, wd_hbm, ina_hbm, outb_hbm,
    downa_hbm, downb_hbm, wh_hbm,
    out_ref, lt_ref, lse_ref,
    back,
    ids, lens, xs, stage, mstage, recv, mrecv, normed, low_g, low_u, hidden, mixed, y, last,
    wgu, wd, ina, outb, downa, downb, wh,
    fin, gathered, wide, stats, own_stats,
    isem, wsem, lsem, rsend, rrecv, msend, mrec, ysend, yrecv,
    fsend, frecv, gsend, grecv, ssend, srecv,
):
    f32 = jnp.float32
    bf16 = jnp.bfloat16
    q = lax.axis_index("req")
    a = lax.axis_index("ad")
    n = n_q * groups
    me = q * groups + a
    seq, width = xs.shape[1:]
    rank = downa.shape[0] // per_dev
    units = wd.shape[0]
    slots = n * groups
    total_req = n * n_req
    barrier = pltpu.get_barrier_semaphore()

    def target(k):
        t = lax.rem(me + k, n)
        return (lax.div(t, groups), lax.rem(t, groups))

    firsts = [
        pltpu.make_async_copy(ids_hbm, ids, isem.at[0]),
        pltpu.make_async_copy(len_hbm, lens, isem.at[1]),
        pltpu.make_async_copy(x_hbm, xs, isem.at[2]),
    ]
    for copy in firsts:
        copy.start()

    def greet(k, carry):
        pl.semaphore_signal(barrier, inc=1, device_id=target(k), device_id_type=MESH)
        return carry

    lax.fori_loop(1, n, greet, 0)
    part = width // 4
    loads = [pltpu.make_async_copy(ina_hbm, ina, wsem.at[0])]
    for j in range(2):
        for c in range(4):
            rows = pl.ds(c * part, part)
            loads.append(
                pltpu.make_async_copy(
                    wgu_hbm.at[j, rows], wgu.at[j, rows], wsem.at[1 + 4 * j + c]
                )
            )
    loads.append(pltpu.make_async_copy(outb_hbm, outb, wsem.at[9]))
    early = len(loads)
    loads.append(pltpu.make_async_copy(downa_hbm, downa, wsem.at[10]))
    loads.append(pltpu.make_async_copy(downb_hbm, downb, wsem.at[11]))
    for c in range(2):
        rows = pl.ds(c * (units // 2), units // 2)
        loads.append(pltpu.make_async_copy(wd_hbm.at[rows], wd.at[rows], wsem.at[12 + c]))
    later = len(loads)
    loads.append(pltpu.make_async_copy(wh_hbm, wh, wsem.at[14]))
    for copy in firsts:
        copy.wait()
    for copy in loads:
        copy.start()

    line = lax.broadcasted_iota(jnp.int32, (8, 128), 0)

    def fill(k, carry):
        h = lax.rem(a + k, groups)
        pick = jnp.int32(-1)
        code = jnp.int32(0)
        size = jnp.int32(0)
        for r in range(n_req):
            i = ids[r]
            hit = lax.div(i, per_dev) == h
            pick = jnp.where(hit, r, pick)
            code = jnp.where(hit, lax.rem(i, per_dev), code)
            size = jnp.where(hit, lens[r], size)
        stage[k] = xs[jnp.maximum(pick, 0)]
        mstage[k] = jnp.where(line == 0, code, jnp.where(line == 1, size, pick))
        return carry

    lax.fori_loop(0, groups, fill, 0)
    pl.semaphore_wait(barrier, n - 1)

    def row_copy(k):
        return pltpu.make_async_remote_copy(
            src_ref=stage.at[k], dst_ref=recv.at[k],
            send_sem=rsend.at[k], recv_sem=rrecv.at[k],
            device_id=(q, lax.rem(a + k, groups)), device_id_type=MESH,
        )

    def meta_copy(k):
        return pltpu.make_async_remote_copy(
            src_ref=mstage.at[k], dst_ref=mrecv.at[k],
            send_sem=msend.at[k], recv_sem=mrec.at[k],
            device_id=(q, lax.rem(a + k, groups)), device_id_type=MESH,
        )

    def back_copy(k):
        return pltpu.make_async_remote_copy(
            src_ref=y.at[k], dst_ref=back.at[a],
            send_sem=ysend.at[k], recv_sem=yrecv.at[k],
            device_id=(q, lax.rem(a + groups - k, groups)), device_id_type=MESH,
        )

    def start_rows(k, carry):
        meta_copy(k).start()
        row_copy(k).start()
        return carry

    lax.fori_loop(1, groups, start_rows, 0)
    recv[0] = stage[0]
    mrecv[0] = mstage[0]
    gain = gain_ref[...].reshape(1, width)
    lane = lax.broadcasted_iota(jnp.int32, (seq, per_dev * 2 * rank), 1)
    lane_d = lax.broadcasted_iota(jnp.int32, (seq, per_dev * rank), 1)
    group_of = lax.div(lane, 2 * rank)
    is_gate = lax.rem(lane, 2 * rank) < rank
    row_at = lax.broadcasted_iota(jnp.int32, (seq, width), 0)
    per = groups // CHUNKS
    size = per * seq
    tile_f = 512
    tile_d = width // 3
    own_back = pltpu.make_async_copy(y.at[0], back.at[a], lsem)

    for chunk in range(CHUNKS):
        mine = range(chunk * per, (chunk + 1) * per)
        for s in mine:
            if s > 0:
                meta_copy(s).wait_recv()
                row_copy(s).wait_recv()
            v = recv[s].astype(f32)
            mean_sq = jnp.mean(v * v, axis=-1, keepdims=True)
            at = (s - chunk * per) * seq
            normed[at : at + seq, :] = (v * lax.rsqrt(mean_sq + epsilon) * gain).astype(bf16)
        if chunk == 0:
            for copy in loads[:early]:
                copy.wait()
        low = lax.dot_general(normed[...], ina[...], NT, preferred_element_type=f32)
        for s in mine:
            at = (s - chunk * per) * seq
            here = group_of == mrecv[s, 0:1, : lane.shape[1]]
            piece = low[at : at + seq]
            low_g[at : at + seq, :] = jnp.where(here & is_gate, piece, 0.0).astype(bf16)
            low_u[at : at + seq, :] = jnp.where(
                here & jnp.logical_not(is_gate), piece, 0.0
            ).astype(bf16)

        def units_step(j, carry):
            cols = pl.ds(pl.multiple_of(j * tile_f, tile_f), tile_f)
            gate = jnp.dot(normed[...], wgu[0, :, cols], preferred_element_type=f32)
            gate = gate + jnp.dot(low_g[...], outb[:, cols], preferred_element_type=f32)
            up = jnp.dot(normed[...], wgu[1, :, cols], preferred_element_type=f32)
            up = up + jnp.dot(low_u[...], outb[:, cols], preferred_element_type=f32)
            hidden[:, cols] = (gate / (1.0 + jnp.exp(-gate)) * up).astype(bf16)
            return carry

        lax.fori_loop(0, units // tile_f, units_step, 0)
        if chunk == 0:
            for copy in loads[early:later]:
                copy.wait()
        low_d = lax.dot_general(hidden[...], downa[...], NT, preferred_element_type=f32)
        pieces = []
        for s in mine:
            at = (s - chunk * per) * seq
            here = lax.div(lane_d, rank) == mrecv[s, 0:1, : lane_d.shape[1]]
            pieces.append(jnp.where(here, low_d[at : at + seq], 0.0))
        low_d = jnp.concatenate(pieces, axis=0).astype(bf16)
        low_g[:, : lane_d.shape[1]] = low_d

        def width_step(j, carry):
            cols = pl.ds(pl.multiple_of(j * tile_d, tile_d), tile_d)
            mixed[:, cols] = jnp.dot(
                hidden[...], wd[:, cols], preferred_element_type=f32
            ) + jnp.dot(
                low_g[:, : lane_d.shape[1]], downb[:, cols], preferred_element_type=f32
            )
            return carry

        lax.fori_loop(0, width // tile_d, width_step, 0)
        for s in mine:
            at = (s - chunk * per) * seq
            length = mrecv[s, 1:2, 0:1]
            total = recv[s].astype(f32) + mixed[at : at + seq, :]
            out = jnp.where(row_at < length, total, 0.0).astype(bf16)
            y[s] = out
            last[s : s + 1, :width] = jnp.sum(
                jnp.where(row_at == length - 1, out.astype(f32), 0.0), axis=0, keepdims=True
            )
            last[s : s + 1, width:] = mrecv[s, 2:3, :].astype(f32)
        if chunk < CHUNKS - 1:
            for s in mine:
                if s > 0:
                    back_copy(s).start()
                else:
                    own_back.start()

    rows = last[:, :width]
    mean_sq = jnp.mean(rows * rows, axis=-1, keepdims=True)
    fin[:, :width] = (rows * lax.rsqrt(mean_sq + epsilon) * fgain_ref[...].reshape(1, width)).astype(bf16)
    fin[:, width:] = last[:, width:].astype(bf16)
    gathered[me] = fin[...]

    half = n // 2
    pairs = n_q // 2
    core = lax.rem(q, 2)
    sibling = (q + 1 - 2 * core, a)
    place_me = lax.div(q, 2) * groups + a

    def far(k):
        t = lax.rem(place_me + k, half)
        return (2 * lax.div(t, groups) + core, lax.rem(t, groups))

    def fin_copy(k):
        return pltpu.make_async_remote_copy(
            src_ref=fin, dst_ref=gathered.at[me],
            send_sem=fsend.at[k], recv_sem=frecv.at[k],
            device_id=far(k), device_id_type=MESH,
        )

    def pass_on(k):
        t = lax.rem(place_me + half - k, half)
        origin = (2 * lax.div(t, groups) + core) * groups + lax.rem(t, groups)
        return pltpu.make_async_remote_copy(
            src_ref=gathered.at[origin], dst_ref=gathered.at[origin],
            send_sem=gsend.at[k], recv_sem=grecv.at[k],
            device_id=sibling, device_id_type=MESH,
        )

    def stat_copy(k):
        return pltpu.make_async_remote_copy(
            src_ref=own_stats, dst_ref=stats.at[me],
            send_sem=ssend.at[k], recv_sem=srecv.at[k],
            device_id=target(k), device_id_type=MESH,
        )

    def each(low_k, high_k, action):
        def body(k, carry):
            action(k)
            return carry
        lax.fori_loop(low_k, high_k, body, 0)

    each(1, half, lambda k: fin_copy(k).start())
    pass_on(0).start()
    for s in range((CHUNKS - 1) * per, groups):
        if s > 0:
            back_copy(s).start()
        else:
            own_back.start()

    def relay(k):
        fin_copy(k).wait_recv()
        pass_on(k).start()

    each(1, half, relay)
    each(0, half, lambda k: pass_on(k).wait_recv())

    def widen(d):
        at = pl.multiple_of(d * groups, 8)
        wide[pl.ds(at, groups), :] = gathered[d].astype(f32)

    each(0, n, widen)
    picked = jnp.transpose(wide[:, width:])[0:1, :].astype(jnp.int32)
    slot = lax.broadcasted_iota(jnp.int32, (1, slots), 1)
    device = lax.div(slot, groups)
    holder = lax.rem(device, groups)
    source = lax.rem(holder + groups - lax.rem(slot, groups), groups)
    row_id = (lax.div(device, groups) * groups + source) * n_req + picked
    row_id = jnp.where(picked >= 0, row_id, -1)
    want = lax.broadcasted_iota(jnp.int32, (total_req, slots), 0)
    place = jnp.where(want == row_id, 1.0, 0.0).astype(bf16)
    ordered = jnp.dot(
        place, wide[:, :width].astype(bf16), preferred_element_type=f32
    ).astype(bf16)
    loads[later].wait()
    logits = lax.dot_general(wh[...], ordered, NT, preferred_element_type=f32)
    lt_ref[...] = logits
    top = jnp.max(logits, axis=0, keepdims=True)
    own_stats[0:1, :] = top
    own_stats[1:2, :] = jnp.sum(jnp.exp(logits - top), axis=0, keepdims=True)
    each(1, n, lambda k: stat_copy(k).start())
    stats[me] = own_stats[...]

    def settle(k):
        row_copy(k).wait_send()
        meta_copy(k).wait_send()
        back_copy(k).wait()

    each(1, groups, settle)
    own_back.wait()
    for r in range(n_req):
        out_ref[r] = back[lax.div(ids[r], per_dev)]
    each(1, half, lambda k: fin_copy(k).wait_send())
    each(0, half, lambda k: pass_on(k).wait_send())
    each(1, n, lambda k: stat_copy(k).wait())
    tops = stats[:, 0, :]
    best = jnp.max(tops, axis=0, keepdims=True)
    total = jnp.sum(stats[:, 1, :] * jnp.exp(tops - best), axis=0, keepdims=True)
    lse_ref[...] = best + jnp.log(total)


def local(
    residual,
    lengths,
    adapter_ids,
    ffn_gain,
    w_gate_up,
    w_down,
    adapter_input_first,
    ad_out_b,
    ad_down_a,
    adapter_down_second,
    final_gain,
    head_weight,
):
    n_req, seq, width = residual.shape
    groups = lax.axis_size("ad")
    n_q = lax.axis_size("req")
    n = n_q * groups
    per_dev = adapter_input_first.shape[0]
    rank = ad_down_a.shape[1]
    units = w_down.shape[0]
    shard = head_weight.shape[1]
    total_req = n * n_req
    rows = groups // CHUNKS * seq
    f32 = jnp.float32
    bf16 = jnp.bfloat16
    ina = adapter_input_first.reshape(per_dev * 2 * rank, width)
    outb = ad_out_b.reshape(per_dev * 2 * rank, units)
    downa = ad_down_a.reshape(per_dev * rank, units)
    downb = adapter_down_second.reshape(per_dev * rank, width)
    head_t = head_weight.T
    dma = pltpu.SemaphoreType.DMA
    vm = pltpu.VMEM
    layer_out, logits_t, lse = pl.pallas_call(
        functools.partial(layer_kernel, n_q, groups, per_dev, n_req),
        out_shape=(
            jax.ShapeDtypeStruct((n_req, seq, width), bf16),
            jax.ShapeDtypeStruct((shard, total_req), f32),
            jax.ShapeDtypeStruct((1, total_req), f32),
        ),
        in_specs=[ANY_SPEC] * 3 + [VMEM_SPEC] * 2 + [ANY_SPEC] * 7,
        out_specs=(VMEM_SPEC,) * 3,
        scratch_shapes=[
            vm((groups, seq, width), bf16),
            pltpu.SMEM((n_req,), jnp.int32),
            pltpu.SMEM((n_req,), jnp.int32),
            vm((n_req, seq, width), bf16),
            vm((groups, seq, width), bf16),
            vm((groups, 8, 128), jnp.int32),
            vm((groups, seq, width), bf16),
            vm((groups, 8, 128), jnp.int32),
            vm((rows, width), bf16),
            vm((rows, per_dev * 2 * rank), bf16),
            vm((rows, per_dev * 2 * rank), bf16),
            vm((rows, units), bf16),
            vm((rows, width), f32),
            vm((groups, seq, width), bf16),
            vm((groups, width + 128), f32),
            vm(w_gate_up.shape, bf16),
            vm(w_down.shape, bf16),
            vm(ina.shape, bf16),
            vm(outb.shape, bf16),
            vm(downa.shape, bf16),
            vm(downb.shape, bf16),
            vm(head_t.shape, bf16),
            vm((groups, width + 128), bf16),
            vm((n, groups, width + 128), bf16),
            vm((n * groups, width + 128), f32),
            vm((n, 2, total_req), f32),
            vm((2, total_req), f32),
            dma((3,)), dma((15,)), dma(()),
            dma((groups,)), dma((groups,)), dma((groups,)), dma((groups,)),
            dma((groups,)), dma((groups,)),
            dma((n // 2,)), dma((n // 2,)), dma((n // 2,)), dma((n // 2,)),
            dma((n,)), dma((n,)),
        ],
        compiler_params=pltpu.CompilerParams(
            collective_id=0, has_side_effects=True, vmem_limit_bytes=60 << 20
        ),
    )(
        adapter_ids, lengths, residual, ffn_gain, final_gain, w_gate_up, w_down,
        ina, outb, downa, downb, head_t,
    )
    return layer_out, (logits_t - lse).T


def solution(mesh):
    in_specs = (
        P(("req", "ad"), None, None),
        P(("req", "ad")),
        P(("req", "ad")),
        P(),
        P(),
        P(),
        P("ad", None, None),
        P("ad", None, None, None),
        P("ad", None, None),
        P("ad", None, None),
        P(),
        P(None, ("req", "ad")),
    )
    out_specs = (P(("req", "ad"), None, None), P(None, ("req", "ad")))
    return jax.shard_map(local, mesh=mesh, in_specs=in_specs, out_specs=out_specs, check_vma=False)
```
